32 devices in a mesh: groups: 2 (over y), seq: 4 (over z), head: 2 (over x), sub: 2 (over core).
Axes of the slice: x: 2, y: 2, z: 4, core: 2. Of those that a mesh axis runs over, the one named last changes fastest.
Arguments:
- queries: bfloat16 [1024, 4096], P(('groups', 'seq'), ('head', 'sub')), parts along dimension 0, may hold values from -6 to 6
- keys: bfloat16 [1024, 4096], P(('groups', 'seq'), ('head', 'sub')), parts along dimension 0, may hold values from -6 to 6
- values: bfloat16 [1024, 4096], P(('groups', 'seq'), ('head', 'sub')), parts along dimension 0, may hold values from -6 to 6
- level_index: int32 [1024, 21], P(('groups', 'seq')), parts along dimension 0, may hold values from 0 to 15
- level_table: float32 [16, 32], P(None, ('head', 'sub')), may hold values from 0.01 to 0.1
- out_weight: bfloat16 [4096, 2048], P(('head', 'sub')), may hold values from -0.09375 to 0.09375
- residual: bfloat16 [1024, 2048], P(('groups', 'seq', 'sub')), parts along dimension 0, may hold values from -6 to 6
- norm_gain: float32 [2048], replicated, may hold values from 0.5 to 1.5
- expert_ids: int32 [1024, 8], P(('groups', 'seq', 'sub')), parts along dimension 0, may hold values from 0 to 63, as said below
- expert_slots: int32 [1024, 8], P(('groups', 'seq', 'sub')), parts along dimension 0, may hold values from -1 to 11, as said below
- route_weight: float32 [1024, 8], P(('groups', 'seq', 'sub')), parts along dimension 0, may hold values from 0.6 to 1
- w_gate_up: bfloat16 [64, 2048, 2, 768], P(('seq', 'sub'), None, None, 'head'), may hold values from -0.125 to 0.125
- w_down: bfloat16 [64, 768, 2048], P(('seq', 'sub'), 'head'), may hold values from -0.21875 to 0.21875
Outputs:
- layer_out: bfloat16 [1024, 2048], P(('groups', 'seq', 'sub'), 'head'), parts along dimension 0
The draws below stay inside these ranges and needn't reach their ends.
There are 2 independent parts, one for each index of `groups`. The reference program is written for one: setup_inputs(seed, part) draws one part's arguments, and reference() takes and returns one part's arrays. A program takes and returns all parts, laid end to end along the dimension named above; an argument that names none is the same for every part. Nothing has to cross between parts.
Inputs may be any that keep to these rules, and one draw needn't show every extreme that they name: `expert_ids`: the 8 ids of a token are different. `expert_slots`: -1 marks a dropped pair. Within an aligned block of 64 tokens, kept pairs that name the same expert have different slots; in every block some expert has all 12 slots taken.
All inputs are finite; a program needn't handle non-finite values.
Results may differ from the reference program's by a relative error of at most 0.018.
Values may be sent and summed in bfloat16 or wider, within the bound.
No kernel may reach another device: no remote copies, remote signals or barrier semaphores. Data moves between devices by JAX's collectives and lax.ppermute only.
A program may use at most 128 MiB of HBM per device.

```python
import math
import jax
import jax.numpy as jnp
from jax import lax

D = 2048
HEADS = 32
HEAD_DIM = 128
FF_EXP = 768
EXPERTS = 64
TOPK = 8
LEVELS = 21
TABLE = 16
STRETCH = 128
TOKENS = 512
TOK_MOE = 64
MEAN_LOAD = 8
CAP = 12
HID_PART = 384
LOCAL_LEVELS = 8
SEQ_BITS = 2
N_SEQ = 4
N_HEAD = 2


def route_tables(key):
    base_key = jax.random.fold_in(key, 7)
    hot_expert = jax.random.randint(jax.random.fold_in(base_key, 11), (), 0, EXPERTS)
    block_count = TOKENS // TOK_MOE

    def one_block(block_key):
        subkeys = jax.random.split(block_key, 6)
        expert_order = jax.random.permutation(subkeys[0], EXPERTS)
        position = jnp.zeros((EXPERTS,), jnp.int32).at[expert_order].set(jnp.arange(EXPERTS, dtype=jnp.int32))
        hot_position = position[hot_expert]
        position = jnp.where(position < hot_position, position + 1, position)
        position = position.at[hot_expert].set(0)
        full_count = jax.random.randint(subkeys[1], (), 7 * EXPERTS // 16, EXPERTS // 2 + 1)
        surplus = MEAN_LOAD + (full_count - 1) * (CAP - MEAN_LOAD)
        rest_count = EXPERTS - full_count
        base_cut = surplus // rest_count
        extra_cut = surplus % rest_count
        rest_rank = position - full_count
        cut = base_cut + (rest_rank < extra_cut).astype(jnp.int32)
        swing_size = jax.random.randint(subkeys[2], (EXPERTS // 2,), 0, MEAN_LOAD // 4 + 1)
        pair_swing = swing_size[position // 2]
        paired = position - position % 2 >= full_count
        swing_sign = 1 - 2 * (position % 2)
        swing = jnp.where(paired, swing_sign * pair_swing, 0)
        counts = jnp.where(position == 0, 2 * MEAN_LOAD, jnp.where(position < full_count, CAP, MEAN_LOAD - cut + swing))
        layout = jax.random.permutation(subkeys[3], EXPERTS)
        laid_counts = counts[layout]
        end_marks = jnp.cumsum(laid_counts)
        entry = jnp.arange(TOK_MOE * TOPK, dtype=jnp.int32)
        bucket = jnp.sum((entry[:, None] >= end_marks[None, :]).astype(jnp.int32), axis=1)
        labels = layout[bucket]
        rank_within = entry - (end_marks - laid_counts)[bucket]
        shuffle = jax.random.permutation(subkeys[4], TOK_MOE)
        token_slot = shuffle[entry % TOK_MOE]
        column = entry // TOK_MOE
        scores = jax.random.randint(subkeys[5], (EXPERTS, CAP), 0, 1 << 20) * CAP + jnp.arange(CAP, dtype=jnp.int32)[None, :]
        slot_order = jnp.argsort(scores, axis=1).astype(jnp.int32)
        slot_values = jnp.where(rank_within < CAP, slot_order[labels, jnp.minimum(rank_within, CAP - 1)], -1)
        id_values = jnp.zeros((TOK_MOE, TOPK), jnp.int32).at[token_slot, column].set(labels)
        slot_table = jnp.zeros((TOK_MOE, TOPK), jnp.int32).at[token_slot, column].set(slot_values)
        return (id_values, slot_table)
    block_keys = jax.vmap(lambda index: jax.random.fold_in(base_key, index))(jnp.arange(block_count, dtype=jnp.int32))
    id_values, slot_table = jax.vmap(one_block)(block_keys)
    return (id_values.reshape(TOKENS, TOPK), slot_table.reshape(TOKENS, TOPK))


def draw_expert_ids(key, part):
    return route_tables(key)[0]


def draw_expert_slots(key, part):
    return route_tables(key)[1]


def place_ends(entries, own_key, least, largest):
    longest = entries.shape.index(max(entries.shape))
    spots = []
    for shift in (0, 1):
        where = [jax.random.randint(jax.random.fold_in(own_key, axis), (), 0, length) for axis, length in enumerate(entries.shape)]
        where[longest] = (where[longest] + shift) % entries.shape[longest]
        spots.append(tuple(where))
    return entries.at[spots[0]].set(least).at[spots[1]].set(largest)


def steps_of(rng, shape, cuts, least, top_value):
    loudness, own = 1.0, jax.random.fold_in(rng, 6)
    for dim, blocks in cuts:
        steps = jnp.exp(jax.random.uniform(jax.random.fold_in(own, dim), (blocks,), jnp.float32, least / len(cuts), top_value / len(cuts)))
        loudness = loudness * jnp.repeat(steps, shape[dim] // blocks).reshape([-1 if axis == dim else 1 for axis in range(len(shape))])
    return loudness


def noise(own_key, extent, spread, reach, cuts=(), held_as=jnp.bfloat16):
    factor_of = steps_of(own_key, extent, cuts, -0.22, 0.18) if cuts else 1.0
    result = jax.random.normal(own_key, extent, jnp.float32) * spread * factor_of
    return jnp.minimum(jnp.maximum(result, -reach), reach).astype(held_as)


def setup_inputs(seed: int = 0, part: int = 0) -> dict:
    key_list = jax.random.split(jax.random.key(seed), 14)
    part_keys = jax.random.split(jax.random.fold_in(key_list[13], part), 14)
    return {
        "queries": noise(part_keys[0], (TOKENS, HEADS * HEAD_DIM), 1.0, 6.0, ((0, 4), (1, 4))),
        "keys": noise(part_keys[1], (TOKENS, HEADS * HEAD_DIM), 1.0, 6.0, ((0, 4), (1, 4))),
        "values": noise(part_keys[2], (TOKENS, HEADS * HEAD_DIM), 1.0, 6.0, ((0, 4), (1, 4))),
        "level_index": place_ends(jax.random.randint(part_keys[3], (TOKENS, LEVELS), 0, TABLE), jax.random.fold_in(part_keys[3], 1), 0, TABLE - 1).astype(jnp.int32),
        "level_table": jnp.clip(jnp.exp(math.log(0.1) - 2.3025851 * jax.random.uniform(key_list[4], (TABLE, HEADS), jnp.float32) ** steps_of(key_list[4], (TABLE, HEADS), ((1, 4),), -0.2, 0.2)), 0.01, 0.1),
        "out_weight": noise(key_list[5], (HEADS * HEAD_DIM, D), (HEADS * HEAD_DIM) ** -0.5, 0.09375, ((0, 4),)),
        "residual": noise(part_keys[6], (TOKENS, D), 1.0, 6.0, ((0, 8),)),
        "norm_gain": jnp.clip(1.0 + 0.1 * jax.random.normal(key_list[7], (D,), jnp.float32), 0.5, 1.5),
        "expert_ids": draw_expert_ids(jax.random.fold_in(jax.random.fold_in(key_list[13], part), 71), part),
        "expert_slots": draw_expert_slots(jax.random.fold_in(jax.random.fold_in(key_list[13], part), 71), part),
        "route_weight": jnp.clip(0.6 + 0.39999998 * jax.random.uniform(part_keys[10], (TOKENS, TOPK), jnp.float32) ** steps_of(part_keys[10], (TOKENS, TOPK), ((0, 8),), -0.2, 0.2), 0.6, 1.0),
        "w_gate_up": noise(key_list[11], (EXPERTS, D, 2, FF_EXP), D ** -0.5, 0.125, ((0, 8), (3, 2))),
        "w_down": noise(key_list[12], (EXPERTS, FF_EXP, D), FF_EXP ** -0.5, 0.21875, ((0, 8), (1, 2))),
    }


def bit_length(numbers, digits):
    counted = jnp.zeros_like(numbers)
    for place_bit in range(digits):
        counted = counted + (numbers >= 1 << place_bit).astype(jnp.int32)
    return counted

def reference(queries, keys, values, level_index, level_table, out_weight, residual, norm_gain, expert_ids, expert_slots, route_weight, w_gate_up, w_down):
    inv_root = HEAD_DIM ** (-0.5)
    query_cube = queries.reshape(N_SEQ, STRETCH, HEADS, HEAD_DIM)
    key_cube = keys.reshape(N_SEQ, STRETCH, HEADS, HEAD_DIM)
    value_cube = values.reshape(N_SEQ, STRETCH, HEADS, HEAD_DIM)
    level_weight = level_table[level_index].reshape(N_SEQ, STRETCH, LEVELS, HEADS)
    states = jnp.einsum('cshd,cshe->chde', key_cube.astype(jnp.float32), value_cube.astype(jnp.float32)).astype(jnp.bfloat16)
    position = jnp.arange(STRETCH, dtype=jnp.int32)
    bit_depth = bit_length(position[:, None] ^ position[None, :], LOCAL_LEVELS)
    causal = position[None, :] <= position[:, None]
    blocks = jnp.arange(N_SEQ, dtype=jnp.int32)
    digits = jnp.arange(SEQ_BITS, dtype=jnp.int32)

    def one_block(block_id):
        query_here = query_cube[block_id].astype(jnp.float32)
        key_here = key_cube[block_id].astype(jnp.float32)
        value_here = value_cube[block_id].astype(jnp.float32)
        weights_here = level_weight[block_id]
        mixed_weights = jnp.zeros((HEADS, STRETCH, STRETCH), jnp.float32)
        for level_id in range(LOCAL_LEVELS):
            mixed_weights = jnp.where((causal & (bit_depth == level_id))[None], jnp.transpose(weights_here[:, level_id, :])[:, :, None], mixed_weights)
        scores = jnp.einsum('thd,shd->hts', query_here, key_here)
        mixed_scores = (scores * mixed_weights).astype(jnp.bfloat16)
        within_block = jnp.einsum('hts,she->the', mixed_scores.astype(jnp.float32), value_here)
        distance = bit_length(block_id ^ blocks, SEQ_BITS) - 1
        select = ((blocks < block_id)[:, None] & (distance[:, None] == digits[None, :])).astype(jnp.float32)
        level_states = jnp.einsum('cj,chde->jhde', select, states.astype(jnp.float32), precision=lax.Precision.HIGHEST).astype(jnp.bfloat16)
        level_reads = jnp.einsum('thd,jhde->tjhe', query_here, level_states.astype(jnp.float32))
        across_blocks = lax.optimization_barrier(jnp.sum(weights_here[:, LOCAL_LEVELS:LOCAL_LEVELS + SEQ_BITS, :, None] * level_reads, axis=1))
        return ((within_block + across_blocks) * inv_root).astype(jnp.bfloat16)
    attended = lax.map(one_block, blocks).reshape(TOKENS, HEADS * HEAD_DIM)
    stream = residual.astype(jnp.float32) + jnp.dot(attended, out_weight, preferred_element_type=jnp.float32)
    mean_square = lax.optimization_barrier(jnp.mean(stream * stream, axis=-1, keepdims=True))
    normed = (stream * lax.rsqrt(mean_square + 1e-06) * norm_gain).astype(jnp.bfloat16)
    block_count = TOKENS // TOK_MOE
    block_span = block_count * CAP
    token_ids = jnp.arange(TOKENS, dtype=jnp.int32)[:, None] + jnp.zeros((1, TOPK), jnp.int32)
    block_ids = token_ids // TOK_MOE
    slot_index = jnp.where(expert_slots >= 0, expert_ids * block_span + block_ids * CAP + expert_slots, EXPERTS * block_span)
    token_table = jnp.full((EXPERTS * block_span,), TOKENS, jnp.int32).at[slot_index.reshape(-1)].set(token_ids.reshape(-1), mode='drop')
    weight_table = jnp.zeros((EXPERTS * block_span,), jnp.float32).at[slot_index.reshape(-1)].set(route_weight.reshape(-1), mode='drop')
    token_table = token_table.reshape(EXPERTS, block_span)
    weight_table = weight_table.reshape(EXPERTS, block_span)

    def one_expert(totals, inputs):
        pair_weight, down_weight, token_row, weight_row = inputs
        row_block = jnp.take(normed, jnp.minimum(token_row, TOKENS - 1), axis=0)
        gate_part = jnp.dot(row_block, pair_weight[:, 0, :], preferred_element_type=jnp.float32)
        up_part = jnp.dot(row_block, pair_weight[:, 1, :], preferred_element_type=jnp.float32)
        active = (jax.nn.silu(gate_part) * up_part).astype(jnp.bfloat16)
        pieces = jnp.einsum('rpf,pfd->prd', active.reshape(block_span, N_HEAD, HID_PART).astype(jnp.float32), down_weight.reshape(N_HEAD, HID_PART, D).astype(jnp.float32)).astype(jnp.bfloat16)
        merged = lax.optimization_barrier(jnp.sum(pieces.astype(jnp.float32), axis=0)) * weight_row[:, None]
        return (totals.at[token_row].add(merged, mode='drop'), None)
    expert_sum = lax.scan(one_expert, jnp.zeros((TOKENS, D), jnp.float32), (w_gate_up, w_down, token_table, weight_table))[0]
    return (stream + expert_sum).astype(jnp.bfloat16)
```

```python
import jax
import jax.numpy as jnp
from jax import lax
from jax.experimental import pallas as pl
from jax.experimental.pallas import tpu as pltpu
from jax.sharding import PartitionSpec as P

D = 2048
HEAD_DIM = 128
EXPERTS = 64
TOPK = 8
LOCAL_LEVELS = 8


def swapped(value, axis, distance):
    mask = 2**distance
    pairs = [(source, source ^ mask) for source in range(lax.axis_size(axis))]
    return lax.ppermute(value, axis, pairs)


def moved(value, axis, distance):
    size = lax.axis_size(axis)
    pairs = [(source, (source + distance) % size) for source in range(size)]
    return lax.ppermute(value, axis, pairs)


def expert_kernel(rows_ref, gate_up_ref, down_ref, scale_ref, out_ref):
    pair = jnp.swapaxes(gate_up_ref[0], 0, 1)
    rows = rows_ref[0]
    gate = jnp.dot(rows, pair[0], preferred_element_type=jnp.float32)
    up = jnp.dot(rows, pair[1], preferred_element_type=jnp.float32)
    active = (gate / (1.0 + jnp.exp(-gate)) * up).astype(jnp.bfloat16)
    piece = jnp.dot(active, down_ref[0], preferred_element_type=jnp.float32)
    out_ref[0] = (piece * scale_ref[0]).astype(jnp.bfloat16)


def run_experts(rows, w_gate_up, w_down, scale):
    experts, count, width = rows.shape
    hidden = w_down.shape[1]
    return pl.pallas_call(
        expert_kernel,
        grid=(experts,),
        in_specs=[
            pl.BlockSpec((1, count, width), lambda e: (e, 0, 0)),
            pl.BlockSpec((1, width, 2, hidden), lambda e: (e, 0, 0, 0)),
            pl.BlockSpec((1, hidden, width), lambda e: (e, 0, 0)),
            pl.BlockSpec((1, count, 1), lambda e: (e, 0, 0)),
        ],
        out_specs=pl.BlockSpec((1, count, width), lambda e: (e, 0, 0)),
        out_shape=jax.ShapeDtypeStruct(rows.shape, jnp.bfloat16),
    )(rows, w_gate_up, w_down, scale)


def bit_length(numbers, digits):
    counted = jnp.zeros_like(numbers)
    for place_bit in range(digits):
        counted = counted + (numbers >= 1 << place_bit).astype(jnp.int32)
    return counted


def on_device(
    queries,
    keys,
    values,
    level_index,
    level_table,
    out_weight,
    residual,
    norm_gain,
    expert_ids,
    expert_slots,
    route_weight,
    w_gate_up,
    w_down,
):
    bf16, f32 = jnp.bfloat16, jnp.float32
    n_seq, n_head, n_sub = (lax.axis_size(name) for name in ("seq", "head", "sub"))
    my_seq, my_head, my_sub = (lax.axis_index(name) for name in ("seq", "head", "sub"))
    my_tokens = residual.shape[0]
    route = jnp.concatenate(
        [expert_ids.astype(f32), expert_slots.astype(f32), route_weight], axis=1
    ).T
    routes = [route] + [moved(route, "seq", hop) for hop in range(1, n_seq)]
    routes = jnp.concatenate(routes, axis=1)
    routes = jnp.concatenate([routes] + [moved(routes, "sub", hop) for hop in range(1, n_sub)], axis=1)
    block_len = queries.shape[0]
    heads_here = queries.shape[1] // HEAD_DIM
    inv_root = HEAD_DIM ** (-0.5)
    query_cube = queries.reshape(block_len, heads_here, HEAD_DIM)
    key_cube = keys.reshape(block_len, heads_here, HEAD_DIM)
    value_cube = values.reshape(block_len, heads_here, HEAD_DIM)
    table_rows = level_table.shape[0]
    lookup = (
        level_index[:, :, None] == jnp.arange(table_rows, dtype=jnp.int32)[None, None, :]
    ).astype(jnp.float32)
    level_weight = jnp.einsum("tlr,rh->tlh", lookup, level_table, precision=lax.Precision.HIGHEST)
    block_state = jnp.einsum(
        "shd,she->hde", key_cube, value_cube, preferred_element_type=jnp.float32
    ).astype(jnp.bfloat16)
    seq_bits = lax.axis_size("seq").bit_length() - 1
    my_block = lax.axis_index("seq")
    running = block_state.astype(jnp.float32)
    levels_found = []
    for place_bit in range(seq_bits):
        partner = swapped(running.astype(jnp.bfloat16), "seq", place_bit).astype(running.dtype)
        owned_bit = (my_block >> place_bit & 1).astype(jnp.float32)
        levels_found.append(partner * owned_bit)
        running = running + partner
    stacked = jnp.stack(levels_found)
    level_states = stacked.astype(jnp.bfloat16)
    position = jnp.arange(block_len, dtype=jnp.int32)
    bit_depth = bit_length(position[:, None] ^ position[None, :], LOCAL_LEVELS)
    causal = position[None, :] <= position[:, None]
    mixed_weights = jnp.zeros((heads_here, block_len, block_len), jnp.float32)
    for level_id in range(LOCAL_LEVELS):
        mixed_weights = jnp.where(
            (causal & (bit_depth == level_id))[None],
            jnp.transpose(level_weight[:, level_id, :])[:, :, None],
            mixed_weights,
        )
    scores = jnp.einsum("thd,shd->hts", query_cube, key_cube, preferred_element_type=jnp.float32)
    mixed_scores = (scores * mixed_weights).astype(jnp.bfloat16)
    within_block = jnp.einsum(
        "hts,she->the", mixed_scores, value_cube, preferred_element_type=jnp.float32
    )
    level_reads = jnp.einsum(
        "thd,jhde->tjhe", query_cube, level_states, preferred_element_type=jnp.float32
    )
    across_blocks = jnp.sum(
        level_weight[:, LOCAL_LEVELS : LOCAL_LEVELS + seq_bits, :, None] * level_reads, axis=1
    )
    attended = (
        ((within_block + across_blocks) * inv_root)
        .astype(jnp.bfloat16)
        .reshape(block_len, heads_here * HEAD_DIM)
    )
    capacity = 3 * (my_tokens * TOPK // EXPERTS) // 2
    exp_here = w_gate_up.shape[0]
    named, slots, weights = jnp.split(routes, 3, axis=0)
    all_tokens = named.shape[1]
    blocks = all_tokens // my_tokens
    first = (my_seq * n_sub + my_sub) * exp_here
    local = (first + jnp.arange(exp_here, dtype=jnp.int32)).astype(f32)
    match = (named[None] == local[:, None, None]) & (slots >= 0)[None]
    block_of = (jnp.arange(all_tokens, dtype=jnp.int32) // my_tokens * capacity).astype(f32)
    place = jnp.sum(jnp.where(match, slots[None] + block_of + 1.0, 0.0), axis=1) - 1.0
    share = jnp.sum(jnp.where(match, weights[None], 0.0), axis=1)
    row = jnp.arange(blocks * capacity, dtype=jnp.int32).astype(f32)
    chosen = place[:, None, :] == row[None, :, None]
    scale = jnp.sum(jnp.where(chosen, share[:, None, :], 0.0), axis=2, keepdims=True)
    pick = chosen.astype(bf16).reshape(exp_here * blocks * capacity, all_tokens)

    partial_value = jnp.dot(attended, out_weight, preferred_element_type=f32)
    by_sub = partial_value.reshape(n_sub, my_tokens, D)
    my_rows = lax.dynamic_index_in_dim(by_sub, my_sub, 0, keepdims=False)
    for hop in range(1, n_sub):
        outgoing = lax.dynamic_index_in_dim(by_sub, (my_sub + hop) % n_sub, 0, keepdims=False)
        my_rows = my_rows + moved(outgoing.astype(bf16), "sub", hop).astype(f32)
    shared = my_rows.astype(bf16)
    total = shared.astype(f32)
    for hop in range(1, n_head):
        total = total + moved(shared, "head", hop).astype(f32)
    stream = residual.astype(f32) + total
    mean_square = jnp.mean(stream * stream, axis=-1, keepdims=True)
    normed = (stream * lax.rsqrt(mean_square + 1e-06) * norm_gain).astype(bf16)

    width = D // n_head
    mine = lax.dynamic_slice_in_dim(normed, my_head * width, width, 1)
    gathered = [normed]
    step = max(1, n_seq // 4)
    for begin in range(1, n_seq, step):
        hops = range(begin, min(begin + step, n_seq))
        part = jnp.concatenate([moved(mine, "seq", hop) for hop in hops], axis=0)
        whole = jnp.zeros((n_head, part.shape[0], width), bf16)
        parts = [part] + [moved(part, "head", side) for side in range(1, n_head)]
        for side, piece in enumerate(parts):
            whole = lax.dynamic_update_index_in_dim(whole, piece, (my_head - side) % n_head, 0)
        gathered.append(jnp.transpose(whole, (1, 0, 2)).reshape(-1, D))
    here = jnp.concatenate(gathered, axis=0)
    picks = jnp.split(pick, n_sub, axis=1)
    rows = jnp.dot(picks[0], here, preferred_element_type=f32)
    for hop in range(1, n_sub):
        rows = rows + jnp.dot(picks[hop], moved(here, "sub", hop), preferred_element_type=f32)
    rows = rows.astype(bf16).reshape(exp_here, blocks * capacity, D)
    pieces = run_experts(rows, w_gate_up, w_down, scale).reshape(-1, D)

    def combined(part):
        return lax.dot_general(part, pieces, (((0,), (0,)), ((), ())), preferred_element_type=f32)

    sent = [moved(combined(picks[hop]).astype(bf16), "sub", -hop) for hop in range(1, n_sub)]
    merged = combined(picks[0])
    for value in sent:
        merged = merged + value.astype(f32)
    by_head = merged.reshape(n_seq, my_tokens, n_head, width)
    expert_sum = 0.0
    for begin in range(0, n_seq, step):
        hops = range(begin, min(begin + step, n_seq))
        group = by_head[begin : hops[-1] + 1]
        own = lax.dynamic_index_in_dim(group, my_head, 2, keepdims=False)
        for side in range(1, n_head):
            away = lax.dynamic_index_in_dim(group, (my_head + side) % n_head, 2, keepdims=False)
            own = own + moved(away.astype(bf16), "head", side).astype(f32)
        for place_in, hop in enumerate(hops):
            value = own[place_in]
            if hop:
                value = moved(value.astype(bf16), "seq", -hop).astype(f32)
            expert_sum = expert_sum + value
    stream_part = lax.dynamic_slice_in_dim(stream, my_head * width, width, 1)
    return (stream_part + expert_sum).astype(bf16)


def solution(mesh):
    return jax.shard_map(
        on_device,
        mesh=mesh,
        in_specs=(
            P(("groups", "seq"), ("head", "sub")),
            P(("groups", "seq"), ("head", "sub")),
            P(("groups", "seq"), ("head", "sub")),
            P(("groups", "seq"), None),
            P(None, ("head", "sub")),
            P(("head", "sub"), None),
            P(("groups", "seq", "sub"), None),
            P(),
            P(("groups", "seq", "sub"), None),
            P(("groups", "seq", "sub"), None),
            P(("groups", "seq", "sub"), None),
            P(("seq", "sub"), None, None, "head"),
            P(("seq", "sub"), "head", None),
        ),
        out_specs=P(("groups", "seq", "sub"), "head"),
        check_vma=False,
    )
```

```python
import functools

import jax
import jax.numpy as jnp
from jax import lax
from jax.experimental import pallas as pl
from jax.experimental.pallas import tpu as pltpu
from jax.sharding import PartitionSpec as P

D = 2048
HEAD_DIM = 128
EXPERTS = 64
TOPK = 8
LOCAL_LEVELS = 8
FUSED_BYTES = 4 << 20

bf16, f32 = jnp.bfloat16, jnp.float32
SMEM = pltpu.MemorySpace.SMEM
VMEM = pltpu.MemorySpace.VMEM


def moved(value, axis, distance):
    size = lax.axis_size(axis)
    pairs = [(source, (source + distance) % size) for source in range(size)]
    return lax.ppermute(value, axis, pairs)


def swapped(value, axis, distance, upward):
    mask = 2**distance
    pairs = [(s, s ^ mask) for s in range(lax.axis_size(axis)) if not (upward and s & mask)]
    return lax.ppermute(value, axis, pairs)


def dot(a, b, contract=((1,), (0,))):
    return lax.dot_general(a, b, (contract, ((), ())), preferred_element_type=f32)


def bit_length(numbers, digits):
    counted = jnp.zeros_like(numbers)
    for place_bit in range(digits):
        counted = counted + (numbers >= 1 << place_bit).astype(jnp.int32)
    return counted


def columns(head):
    return slice(head * HEAD_DIM, (head + 1) * HEAD_DIM)


def looked_up(index, table_ref, head):
    weight = jnp.zeros(index.shape, f32)
    for entry in range(table_ref.shape[0]):
        weight = jnp.where(index == entry, table_ref[entry, head], weight)
    return weight


def state_kernel(keys_ref, values_ref, out_ref):
    for head in range(out_ref.shape[0]):
        span = columns(head)
        out_ref[head] = dot(keys_ref[:, span], values_ref[:, span], ((0,), (0,))).astype(bf16)


def within_kernel(table_ref, queries_ref, keys_ref, values_ref, index_ref, out_ref):
    block = queries_ref.shape[0]
    rows = lax.broadcasted_iota(jnp.int32, (block, block), 0)
    cols = lax.broadcasted_iota(jnp.int32, (block, block), 1)
    depth = jnp.where(cols <= rows, bit_length(rows ^ cols, LOCAL_LEVELS), -1)
    index = index_ref[...]
    for head in range(out_ref.shape[1] // HEAD_DIM):
        span = columns(head)
        weight = looked_up(index, table_ref, head)
        mix = jnp.zeros((block, block), f32)
        for level in range(LOCAL_LEVELS):
            mix = jnp.where(depth == level, weight[:, level : level + 1], mix)
        scores = dot(queries_ref[:, span], keys_ref[:, span], ((1,), (1,)))
        mixed = (scores * mix).astype(bf16)
        out_ref[:, span] = dot(mixed, values_ref[:, span])


def project_kernel(n_levels, table_ref, place_ref, within_ref, queries_ref, index_ref, *rest):
    state_refs = rest[:n_levels]
    weight_ref, own_ref, away_ref, attended_ref = rest[n_levels:]

    @pl.when(pl.program_id(0) == 0)
    def _():
        index = index_ref[...]
        for head in range(queries_ref.shape[1] // HEAD_DIM):
            span = columns(head)
            weight = looked_up(index, table_ref, head)
            total = within_ref[:, span]
            for level in range(n_levels):
                read = dot(queries_ref[:, span], state_refs[level][head])
                column = LOCAL_LEVELS + level
                owned = (place_ref[1] >> level & 1).astype(f32)
                total = total + (weight[:, column : column + 1] * owned) * read
            attended_ref[:, span] = (total * HEAD_DIM ** (-0.5)).astype(bf16)

    tokens = own_ref.shape[0]
    n_sub = away_ref.shape[0] + 1
    my_sub = place_ref[0]
    weight = weight_ref[...]
    for hop in range(n_sub):
        start = pl.multiple_of((my_sub + hop) % n_sub * tokens, tokens)
        value = dot(attended_ref[pl.ds(start, tokens), :], weight)
        if hop:
            away_ref[hop - 1] = value.astype(bf16)
        else:
            own_ref[...] = value


def whole(shape):
    return pl.BlockSpec(shape, lambda *_: (0,) * len(shape))


def scalars():
    return pl.BlockSpec(memory_space=SMEM)


def attention(queries, keys, values, level_index, level_table, out_weight, my_tokens):
    block, width = queries.shape
    heads = width // HEAD_DIM
    n_seq, n_sub = lax.axis_size("seq"), lax.axis_size("sub")
    my_block = lax.axis_index("seq")
    state = pl.pallas_call(
        state_kernel, out_shape=jax.ShapeDtypeStruct((heads, HEAD_DIM, HEAD_DIM), bf16)
    )(keys, values)
    levels = n_seq.bit_length() - 1
    running = state.astype(f32)
    found = []
    for level in range(levels):
        partner = swapped(running.astype(bf16), "seq", level, level == levels - 1)
        found.append(partner)
        running = running + partner.astype(f32)
    within = pl.pallas_call(
        within_kernel,
        in_specs=[scalars()] + [pl.BlockSpec(memory_space=VMEM)] * 4,
        out_shape=jax.ShapeDtypeStruct((block, width), f32),
    )(level_table, queries, keys, values, level_index)
    place = jnp.stack([lax.axis_index("sub"), my_block]).astype(jnp.int32)
    out_width = out_weight.shape[1]
    step = out_width // 4
    return pl.pallas_call(
        functools.partial(project_kernel, levels),
        grid=(out_width // step,),
        in_specs=[
            scalars(),
            scalars(),
            whole((block, width)),
            whole((block, width)),
            whole(level_index.shape),
        ]
        + [whole((heads, HEAD_DIM, HEAD_DIM))] * levels
        + [pl.BlockSpec((width, step), lambda i: (0, i))],
        out_specs=[
            pl.BlockSpec((my_tokens, step), lambda i: (0, i)),
            pl.BlockSpec((n_sub - 1, my_tokens, step), lambda i: (0, 0, i)),
        ],
        out_shape=[
            jax.ShapeDtypeStruct((my_tokens, out_width), f32),
            jax.ShapeDtypeStruct((n_sub - 1, my_tokens, out_width), bf16),
        ],
        scratch_shapes=[pltpu.VMEM((block, width), bf16)],
    )(level_table, place, within, queries, level_index, *found, out_weight)


def swiglu(gate, up):
    return (gate / (1.0 + jnp.exp(-gate)) * up).astype(bf16)


def expert_kernel(rows_ref, gate_up_ref, down_ref, scale_ref, out_ref):
    pair = jnp.swapaxes(gate_up_ref[0], 0, 1)
    rows = rows_ref[0]
    active = swiglu(dot(rows, pair[0]), dot(rows, pair[1]))
    out_ref[0] = (dot(active, down_ref[0]) * scale_ref[0]).astype(bf16)


def run_experts(rows, w_gate_up, w_down, scale):
    experts, count, width = rows.shape
    hidden = w_down.shape[1]
    return pl.pallas_call(
        expert_kernel,
        grid=(experts,),
        in_specs=[
            pl.BlockSpec((1, count, width), lambda e: (e, 0, 0)),
            pl.BlockSpec((1, width, 2, hidden), lambda e: (e, 0, 0, 0)),
            pl.BlockSpec((1, hidden, width), lambda e: (e, 0, 0)),
            pl.BlockSpec((1, count, 1), lambda e: (e, 0, 0)),
        ],
        out_specs=pl.BlockSpec((1, count, width), lambda e: (e, 0, 0)),
        out_shape=jax.ShapeDtypeStruct(rows.shape, bf16),
    )(rows, w_gate_up, w_down, scale)


def routed(named, slots, weights, expert, slot_base):
    match = (named == expert) & (slots >= 0)
    place = jnp.sum(jnp.where(match, slots + slot_base + 1.0, 0.0), axis=-2, keepdims=True) - 1.0
    share = jnp.sum(jnp.where(match, weights, 0.0), axis=-2, keepdims=True)
    return place, share


def fused_kernel(n_pieces, n_head, capacity, where_ref, routes_ref, *rest):
    piece_refs = rest[:n_pieces]
    gate_up_ref, down_ref, out_ref, pick_ref, tokens_ref, rows_ref, scale_ref = rest[n_pieces:]
    step = pl.program_id(0)
    experts = pl.num_programs(0)
    count = scale_ref.shape[1]
    width = tokens_ref.shape[2]

    @pl.when(step == 0)
    def _():
        my_head = where_ref[1]
        size = piece_refs[0].shape[0]
        for number, ref in enumerate(piece_refs):
            block, side = divmod(number, n_head)
            part = (my_head + n_head - side) % n_head
            tokens_ref[part, block * size : (block + 1) * size, :] = ref[...]
        all_tokens = routes_ref.shape[1]
        named = routes_ref[0:TOPK, :]
        slots = routes_ref[TOPK : 2 * TOPK, :]
        weights = routes_ref[2 * TOPK : 3 * TOPK, :]
        lane = lax.broadcasted_iota(jnp.int32, (1, all_tokens), 1)
        slot_base = (lane // size * capacity).astype(f32)
        row = lax.broadcasted_iota(jnp.int32, (count, all_tokens), 0).astype(f32)
        for expert in range(scale_ref.shape[0]):
            name = (where_ref[0] + expert).astype(f32)
            place, share = routed(named, slots, weights, name, slot_base)
            chosen = place == row
            scale_ref[expert] = jnp.sum(jnp.where(chosen, share, 0.0), axis=1, keepdims=True)
            pick_ref[expert * count : (expert + 1) * count, :] = jnp.where(
                chosen, 1.0, 0.0
            ).astype(bf16)
        for part in range(n_head):
            rows_ref[part] = dot(pick_ref[...], tokens_ref[part]).astype(bf16)

    start = pl.multiple_of(step * count, count)
    pair = jnp.swapaxes(gate_up_ref[0], 0, 1)
    gate = up = 0.0
    for part in range(n_head):
        rows = rows_ref[part, pl.ds(start, count), :]
        span = slice(part * width, (part + 1) * width)
        gate = gate + dot(rows, pair[0, span, :])
        up = up + dot(rows, pair[1, span, :])
    piece = (dot(swiglu(gate, up), down_ref[0]) * scale_ref[step]).astype(bf16)
    for part in range(n_head):
        out_ref[part] = piece[:, part * width : (part + 1) * width]


def run_fused(where, routes, pieces, w_gate_up, w_down, n_head, capacity):
    experts, full, _, hidden = w_gate_up.shape
    size, width = pieces[0].shape
    all_tokens = routes.shape[1]
    count = all_tokens // size * capacity
    return pl.pallas_call(
        functools.partial(fused_kernel, len(pieces), n_head, capacity),
        grid=(experts,),
        in_specs=[scalars(), whole(routes.shape)]
        + [whole((size, width))] * len(pieces)
        + [
            pl.BlockSpec((1, full, 2, hidden), lambda e: (e, 0, 0, 0)),
            pl.BlockSpec((1, hidden, full), lambda e: (e, 0, 0)),
        ],
        out_specs=[
            pl.BlockSpec((n_head, count, width), lambda e: (0, e, 0)),
            whole((experts * count, all_tokens)),
        ],
        out_shape=[
            jax.ShapeDtypeStruct((n_head, experts * count, width), bf16),
            jax.ShapeDtypeStruct((experts * count, all_tokens), bf16),
        ],
        scratch_shapes=[
            pltpu.VMEM((n_head, all_tokens, width), bf16),
            pltpu.VMEM((n_head, experts * count, width), bf16),
            pltpu.VMEM((experts, count, 1), f32),
        ],
    )(where, routes, *pieces, w_gate_up, w_down)


def combine_kernel(part_ref, pick_ref, rows_ref, *rest):
    out_ref = rest[-1]
    value = dot(pick_ref[...], rows_ref[0], ((0,), (0,)))
    for ref in rest[:-1]:
        value = value + ref[...].astype(f32)
    out_ref[...] = value.astype(out_ref.dtype)


def run_combine(part, pick, rows, sub, n_sub, extra, dtype):
    total, all_tokens = pick.shape
    tokens = all_tokens // n_sub
    width = rows.shape[2]
    return pl.pallas_call(
        combine_kernel,
        grid_spec=pltpu.PrefetchScalarGridSpec(
            num_scalar_prefetch=1,
            grid=(1,),
            in_specs=[
                pl.BlockSpec((total, tokens), lambda i, part_ref: (0, sub)),
                pl.BlockSpec((1, total, width), lambda i, part_ref: (part_ref[0], 0, 0)),
            ]
            + [whole((tokens, width))] * len(extra),
            out_specs=whole((tokens, width)),
        ),
        out_shape=jax.ShapeDtypeStruct((tokens, width), dtype),
    )(part, pick, rows, *extra)


def on_device(
    queries,
    keys,
    values,
    level_index,
    level_table,
    out_weight,
    residual,
    norm_gain,
    expert_ids,
    expert_slots,
    route_weight,
    w_gate_up,
    w_down,
):
    n_seq, n_head, n_sub = (lax.axis_size(name) for name in ("seq", "head", "sub"))
    my_seq, my_head, my_sub = (lax.axis_index(name) for name in ("seq", "head", "sub"))
    my_tokens = residual.shape[0]
    route = jnp.concatenate(
        [expert_ids.astype(f32), expert_slots.astype(f32), route_weight], axis=1
    ).T
    routes = [route] + [moved(route, "seq", hop) for hop in range(1, n_seq)]
    routes = jnp.concatenate(routes, axis=1)
    routes = jnp.concatenate([routes] + [moved(routes, "sub", hop) for hop in range(1, n_sub)], axis=1)

    my_rows, away = attention(
        queries, keys, values, level_index, level_table, out_weight, my_tokens
    )
    for hop in range(1, n_sub):
        my_rows = my_rows + moved(away[hop - 1], "sub", hop).astype(f32)
    shared = my_rows.astype(bf16)
    total = shared.astype(f32)
    for hop in range(1, n_head):
        total = total + moved(shared, "head", hop).astype(f32)
    stream = residual.astype(f32) + total
    mean_square = jnp.mean(stream * stream, axis=-1, keepdims=True)
    normed = (stream * lax.rsqrt(mean_square + 1e-06) * norm_gain).astype(bf16)

    width = D // n_head
    capacity = 3 * (my_tokens * TOPK // EXPERTS) // 2
    exp_here = w_gate_up.shape[0]
    all_tokens = routes.shape[1]
    first = (my_seq * n_sub + my_sub) * exp_here
    stream_part = lax.dynamic_slice_in_dim(stream, my_head * width, width, 1)

    def part_of(value, side):
        return lax.dynamic_slice_in_dim(value, (my_head - side) % n_head * width, width, 1)

    mine = part_of(normed, 0)
    if all_tokens * D * 2 <= FUSED_BYTES:
        blocks = [[part_of(normed, side) for side in range(n_head)]]
        for hop in range(1, n_seq):
            part = moved(mine, "seq", hop)
            blocks.append([part] + [moved(part, "head", side) for side in range(1, n_head)])
        pieces = [piece for block in blocks for piece in block]
        pieces = pieces + [
            moved(piece, "sub", hop) for hop in range(1, n_sub) for piece in pieces
        ]
        where = jnp.stack([first, my_head]).astype(jnp.int32)
        rows, pick = run_fused(where, routes, pieces, w_gate_up, w_down, n_head, capacity)

        reduced = []
        for side in [*range(1, n_head), 0]:
            part = ((my_head + side) % n_head).astype(jnp.int32).reshape(1)
            extra = [
                moved(run_combine(part, pick, rows, hop, n_sub, [], bf16), "sub", -hop)
                for hop in range(1, n_sub)
            ]
            value = run_combine(part, pick, rows, 0, n_sub, extra, bf16 if side else f32)
            reduced.append(value.reshape(n_seq, my_tokens, width))
        expert_sum = 0.0
        for hop in [*range(1, n_seq), 0]:
            own = reduced[-1][hop]
            for side in range(1, n_head):
                own = own + moved(reduced[side - 1][hop], "head", side).astype(f32)
            if hop:
                own = moved(own.astype(bf16), "seq", -hop).astype(f32)
            expert_sum = expert_sum + own
        return (stream_part + expert_sum).astype(bf16)

    step = max(1, n_seq // 4)
    gathered = [normed]
    for begin in range(1, n_seq, step):
        hops = range(begin, min(begin + step, n_seq))
        part = jnp.concatenate([moved(mine, "seq", hop) for hop in hops], axis=0)
        joined = jnp.zeros((n_head, part.shape[0], width), bf16)
        parts = [part] + [moved(part, "head", side) for side in range(1, n_head)]
        for side, piece in enumerate(parts):
            joined = lax.dynamic_update_index_in_dim(joined, piece, (my_head - side) % n_head, 0)
        gathered.append(jnp.transpose(joined, (1, 0, 2)).reshape(-1, D))
    here = jnp.concatenate(gathered, axis=0)

    named, slots, weights = jnp.split(routes, 3, axis=0)
    count = all_tokens // my_tokens * capacity
    local = (first + jnp.arange(exp_here, dtype=jnp.int32)).astype(f32)
    block_of = (jnp.arange(all_tokens, dtype=jnp.int32) // my_tokens * capacity).astype(f32)
    place, share = routed(named[None], slots[None], weights[None], local[:, None, None], block_of)
    row = jnp.arange(count, dtype=jnp.int32).astype(f32)
    chosen = place == row[None, :, None]
    scale = jnp.sum(jnp.where(chosen, share, 0.0), axis=2, keepdims=True)
    pick = chosen.astype(bf16).reshape(exp_here * count, all_tokens)
    picks = jnp.split(pick, n_sub, axis=1)
    rows = dot(picks[0], here)
    for hop in range(1, n_sub):
        rows = rows + dot(picks[hop], moved(here, "sub", hop))
    rows = rows.astype(bf16).reshape(exp_here, count, D)
    pieces = run_experts(rows, w_gate_up, w_down, scale).reshape(-1, D)

    def combined(part):
        return dot(part, pieces, ((0,), (0,)))

    sent = [moved(combined(picks[hop]).astype(bf16), "sub", -hop) for hop in range(1, n_sub)]
    merged = combined(picks[0])
    for value in sent:
        merged = merged + value.astype(f32)
    by_head = merged.reshape(n_seq, my_tokens, n_head, width)
    expert_sum = 0.0
    for begin in range(0, n_seq, step):
        hops = range(begin, min(begin + step, n_seq))
        group = by_head[begin : hops[-1] + 1]
        own = lax.dynamic_index_in_dim(group, my_head, 2, keepdims=False)
        for side in range(1, n_head):
            away = lax.dynamic_index_in_dim(group, (my_head + side) % n_head, 2, keepdims=False)
            own = own + moved(away.astype(bf16), "head", side).astype(f32)
        for place_in, hop in enumerate(hops):
            value = own[place_in]
            if hop:
                value = moved(value.astype(bf16), "seq", -hop).astype(f32)
            expert_sum = expert_sum + value
    return (stream_part + expert_sum).astype(bf16)


def solution(mesh):
    return jax.shard_map(
        on_device,
        mesh=mesh,
        in_specs=(
            P(("groups", "seq"), ("head", "sub")),
            P(("groups", "seq"), ("head", "sub")),
            P(("groups", "seq"), ("head", "sub")),
            P(("groups", "seq"), None),
            P(None, ("head", "sub")),
            P(("head", "sub"), None),
            P(("groups", "seq", "sub"), None),
            P(),
            P(("groups", "seq", "sub"), None),
            P(("groups", "seq", "sub"), None),
            P(("groups", "seq", "sub"), None),
            P(("seq", "sub"), None, None, "head"),
            P(("seq", "sub"), "head", None),
        ),
        out_specs=P(("groups", "seq", "sub"), "head"),
        check_vma=False,
    )
```

```python
import functools

import jax
import jax.numpy as jnp
from jax import lax
from jax.experimental import pallas as pl
from jax.experimental.pallas import tpu as pltpu
from jax.sharding import PartitionSpec as P

D = 2048
HEAD_DIM = 128
EXPERTS = 64
TOPK = 8
LOCAL_LEVELS = 8
FUSED_BYTES = 4 << 20

bf16, f32 = jnp.bfloat16, jnp.float32
SMEM = pltpu.MemorySpace.SMEM
VMEM = pltpu.MemorySpace.VMEM


def moved(value, axis, distance):
    size = lax.axis_size(axis)
    pairs = [(source, (source + distance) % size) for source in range(size)]
    return lax.ppermute(value, axis, pairs)


def swapped(value, axis, distance, upward):
    mask = 2**distance
    pairs = [(s, s ^ mask) for s in range(lax.axis_size(axis)) if not (upward and s & mask)]
    return lax.ppermute(value, axis, pairs)


def dot(a, b, contract=((1,), (0,))):
    return lax.dot_general(a, b, (contract, ((), ())), preferred_element_type=f32)


def bit_length(numbers, digits):
    counted = jnp.zeros_like(numbers)
    for place_bit in range(digits):
        counted = counted + (numbers >= 1 << place_bit).astype(jnp.int32)
    return counted


def columns(head):
    return slice(head * HEAD_DIM, (head + 1) * HEAD_DIM)


def looked_up(index, table_ref, head):
    weight = jnp.zeros(index.shape, f32)
    for entry in range(table_ref.shape[1]):
        weight = jnp.where(index == float(entry), table_ref[head, entry], weight)
    return weight


def state_kernel(keys_ref, values_ref, out_ref):
    for head in range(out_ref.shape[0]):
        span = columns(head)
        out_ref[head] = dot(keys_ref[:, span], values_ref[:, span], ((0,), (0,))).astype(bf16)


def within_kernel(table_ref, queries_ref, keys_ref, values_ref, index_ref, out_ref, weight_ref):
    block = queries_ref.shape[0]
    heads = queries_ref.shape[1] // HEAD_DIM
    levels = weight_ref.shape[1] // heads
    my_block = lax.axis_index("seq")
    rows = lax.broadcasted_iota(jnp.int32, (block, block), 0)
    cols = lax.broadcasted_iota(jnp.int32, (block, block), 1)
    depth = jnp.where(cols <= rows, bit_length(rows ^ cols, LOCAL_LEVELS), -1)
    index = index_ref[...].astype(f32).T
    for head in range(heads):
        span = columns(head)
        weight = looked_up(index, table_ref, head)
        mix = jnp.zeros((block, block), f32)
        for level in range(LOCAL_LEVELS):
            mix = jnp.where(depth == level, weight[:, level : level + 1], mix)
        scores = dot(queries_ref[:, span], keys_ref[:, span], ((1,), (1,)))
        mixed = (scores * mix).astype(bf16)
        out_ref[:, span] = dot(mixed, values_ref[:, span])
        for level in range(levels):
            owned = (my_block >> level & 1).astype(f32)
            column, slot = LOCAL_LEVELS + level, head * levels + level
            weight_ref[:, slot : slot + 1] = weight[:, column : column + 1] * owned


def project_kernel(n_levels, within_ref, queries_ref, level_ref, *rest):
    state_refs = rest[:n_levels]
    weight_ref, own_ref, away_ref, attended_ref = rest[n_levels:]

    @pl.when(pl.program_id(0) == 0)
    def _():
        for head in range(queries_ref.shape[1] // HEAD_DIM):
            span = columns(head)
            total = within_ref[:, span]
            joined = jnp.concatenate([ref[head] for ref in state_refs], axis=1)
            reads = dot(queries_ref[:, span], joined)
            for level in range(n_levels):
                slot = head * n_levels + level
                total = total + level_ref[:, slot : slot + 1] * reads[:, columns(level)]
            attended_ref[:, span] = (total * HEAD_DIM ** (-0.5)).astype(bf16)

    tokens = own_ref.shape[0]
    n_sub = away_ref.shape[0] + 1
    my_sub = lax.axis_index("sub")
    weight = weight_ref[...]
    for hop in range(n_sub):
        start = pl.multiple_of((my_sub + hop) % n_sub * tokens, tokens)
        value = dot(attended_ref[pl.ds(start, tokens), :], weight)
        if hop:
            away_ref[hop - 1] = value.astype(bf16)
        else:
            own_ref[...] = value


def grant(mebibytes):
    return pltpu.CompilerParams(vmem_limit_bytes=mebibytes << 20)


def whole(shape):
    return pl.BlockSpec(shape, lambda *_: (0,) * len(shape))


def scalars():
    return pl.BlockSpec(memory_space=SMEM)


def attention(queries, keys, values, level_index, level_table, out_weight, my_tokens, route):
    block, width = queries.shape
    heads = width // HEAD_DIM
    n_seq, n_sub = lax.axis_size("seq"), lax.axis_size("sub")
    state = pl.pallas_call(
        state_kernel,
        out_shape=jax.ShapeDtypeStruct((heads, HEAD_DIM, HEAD_DIM), bf16),
        compiler_params=grant(8),
    )(keys, values)
    levels = n_seq.bit_length() - 1
    in_vmem = pl.BlockSpec(memory_space=VMEM)
    within, level_weight = pl.pallas_call(
        within_kernel,
        in_specs=[scalars()] + [in_vmem] * 4,
        out_shape=[
            jax.ShapeDtypeStruct((block, width), f32),
            jax.ShapeDtypeStruct((block, heads * levels), f32),
        ],
        compiler_params=grant(8),
    )(level_table.T, queries, keys, values, level_index.T)
    running = state.astype(f32)
    found = []
    for level in range(levels):
        sent = running.astype(bf16)
        last = level == levels - 1
        if last:
            sent, within, level_weight, route = lax.optimization_barrier(
                (sent, within, level_weight, route)
            )
        partner = swapped(sent, "seq", level, last)
        found.append(partner)
        running = running + partner.astype(f32)
    routes = [route] + [moved(route, "seq", hop) for hop in range(1, n_seq)]
    routes = jnp.concatenate(routes, axis=1)
    routes = jnp.concatenate([routes] + [moved(routes, "sub", hop) for hop in range(1, n_sub)], axis=1)
    found[-1], routes = lax.optimization_barrier((found[-1], routes))
    out_width = out_weight.shape[1]
    step = out_width // 4
    own, away = pl.pallas_call(
        functools.partial(project_kernel, levels),
        grid=(out_width // step,),
        in_specs=[whole((block, width)), whole((block, width)), whole(level_weight.shape)]
        + [whole((heads, HEAD_DIM, HEAD_DIM))] * levels
        + [pl.BlockSpec((width, step), lambda i: (0, i))],
        out_specs=[
            pl.BlockSpec((my_tokens, step), lambda i: (0, i)),
            pl.BlockSpec((n_sub - 1, my_tokens, step), lambda i: (0, 0, i)),
        ],
        out_shape=[
            jax.ShapeDtypeStruct((my_tokens, out_width), f32),
            jax.ShapeDtypeStruct((n_sub - 1, my_tokens, out_width), bf16),
        ],
        scratch_shapes=[pltpu.VMEM((block, width), bf16)],
        compiler_params=grant(12),
    )(within, queries, level_weight, *found, out_weight)
    return own, away, routes


def swiglu(gate, up):
    return (gate / (1.0 + jnp.exp(-gate)) * up).astype(bf16)


def expert_kernel(rows_ref, gate_up_ref, down_ref, scale_ref, out_ref):
    pair = jnp.swapaxes(gate_up_ref[0], 0, 1)
    rows = rows_ref[0]
    active = swiglu(dot(rows, pair[0]), dot(rows, pair[1]))
    out_ref[0] = (dot(active, down_ref[0]) * scale_ref[0]).astype(bf16)


def run_experts(rows, w_gate_up, w_down, scale):
    experts, count, width = rows.shape
    hidden = w_down.shape[1]
    return pl.pallas_call(
        expert_kernel,
        grid=(experts,),
        in_specs=[
            pl.BlockSpec((1, count, width), lambda e: (e, 0, 0)),
            pl.BlockSpec((1, width, 2, hidden), lambda e: (e, 0, 0, 0)),
            pl.BlockSpec((1, hidden, width), lambda e: (e, 0, 0)),
            pl.BlockSpec((1, count, 1), lambda e: (e, 0, 0)),
        ],
        out_specs=pl.BlockSpec((1, count, width), lambda e: (e, 0, 0)),
        out_shape=jax.ShapeDtypeStruct(rows.shape, bf16),
    )(rows, w_gate_up, w_down, scale)


def routed(named, slots, weights, expert, slot_base):
    match = (named == expert) & (slots >= 0)
    place = jnp.sum(jnp.where(match, slots + slot_base + 1.0, 0.0), axis=-2, keepdims=True) - 1.0
    share = jnp.sum(jnp.where(match, weights, 0.0), axis=-2, keepdims=True)
    return place, share


def fused_kernel(n_pieces, n_head, n_sub, capacity, routes_ref, *rest):
    piece_refs = rest[:n_pieces]
    gate_up_ref, down_ref = rest[n_pieces : n_pieces + 2]
    out_refs = rest[n_pieces + 2 : -5]
    pick_ref, tokens_ref, rows_ref, scale_ref, result_ref = rest[-5:]
    step = pl.program_id(0)
    experts, count = scale_ref.shape[0], scale_ref.shape[1]
    width = tokens_ref.shape[2]
    all_tokens = routes_ref.shape[1]
    my_head = lax.axis_index("head")

    @pl.when(step == 0)
    def _():
        first = (lax.axis_index("seq") * n_sub + lax.axis_index("sub")) * experts
        size = piece_refs[0].shape[0]
        for number, ref in enumerate(piece_refs):
            block, side = divmod(number, n_head)
            part = (my_head + n_head - side) % n_head
            tokens_ref[part, block * size : (block + 1) * size, :] = ref[...]
        named = routes_ref[0:TOPK, :]
        slots = routes_ref[TOPK : 2 * TOPK, :]
        weights = routes_ref[2 * TOPK : 3 * TOPK, :]
        lane = lax.broadcasted_iota(jnp.int32, (1, all_tokens), 1)
        slot_base = (lane // size * capacity).astype(f32)
        row = lax.broadcasted_iota(jnp.int32, (count, all_tokens), 0).astype(f32)
        for expert in range(experts):
            name = (first + expert).astype(f32)
            place, share = routed(named, slots, weights, name, slot_base)
            chosen = place == row
            scale_ref[expert] = jnp.sum(jnp.where(chosen, share, 0.0), axis=1, keepdims=True)
            pick_ref[expert * count : (expert + 1) * count, :] = jnp.where(
                chosen, 1.0, 0.0
            ).astype(bf16)
        for part in range(n_head):
            rows_ref[part] = dot(pick_ref[...], tokens_ref[part]).astype(bf16)

    start = pl.multiple_of(step * count, count)
    pair = jnp.swapaxes(gate_up_ref[0], 0, 1)
    gate = up = 0.0
    for part in range(n_head):
        rows = rows_ref[part, pl.ds(start, count), :]
        span = slice(part * width, (part + 1) * width)
        gate = gate + dot(rows, pair[0, span, :])
        up = up + dot(rows, pair[1, span, :])
    piece = (dot(swiglu(gate, up), down_ref[0]) * scale_ref[step]).astype(bf16)
    for part in range(n_head):
        result_ref[part, pl.ds(start, count), :] = piece[:, part * width : (part + 1) * width]

    @pl.when(step == experts - 1)
    def _():
        tokens = all_tokens // n_sub
        for number, ref in enumerate(out_refs):
            hop, side = divmod(number, n_head)
            part = (my_head + side) % n_head
            pick = pick_ref[:, hop * tokens : (hop + 1) * tokens]
            ref[...] = dot(pick, result_ref[part], ((0,), (0,))).astype(ref.dtype)


def run_fused(routes, pieces, w_gate_up, w_down, n_head, n_sub, capacity):
    experts, full, _, hidden = w_gate_up.shape
    size, width = pieces[0].shape
    all_tokens = routes.shape[1]
    tokens = all_tokens // n_sub
    count = all_tokens // size * capacity
    dtypes = [f32] * n_head + [bf16] * (n_head * (n_sub - 1))
    return pl.pallas_call(
        functools.partial(fused_kernel, len(pieces), n_head, n_sub, capacity),
        grid=(experts,),
        in_specs=[whole(routes.shape)]
        + [whole((size, width))] * len(pieces)
        + [
            pl.BlockSpec((1, full, 2, hidden), lambda e: (e, 0, 0, 0)),
            pl.BlockSpec((1, hidden, full), lambda e: (e, 0, 0)),
        ],
        out_specs=[whole((tokens, width))] * len(dtypes),
        out_shape=[jax.ShapeDtypeStruct((tokens, width), dtype) for dtype in dtypes],
        scratch_shapes=[
            pltpu.VMEM((experts * count, all_tokens), bf16),
            pltpu.VMEM((n_head, all_tokens, width), bf16),
            pltpu.VMEM((n_head, experts * count, width), bf16),
            pltpu.VMEM((experts, count, 1), f32),
            pltpu.VMEM((n_head, experts * count, width), bf16),
        ],
        compiler_params=grant(44),
    )(routes, *pieces, w_gate_up, w_down)


def on_device(
    queries,
    keys,
    values,
    level_index,
    level_table,
    out_weight,
    residual,
    norm_gain,
    expert_ids,
    expert_slots,
    route_weight,
    w_gate_up,
    w_down,
):
    n_seq, n_head, n_sub = (lax.axis_size(name) for name in ("seq", "head", "sub"))
    my_seq, my_head, my_sub = (lax.axis_index(name) for name in ("seq", "head", "sub"))
    my_tokens = residual.shape[0]
    route = jnp.concatenate(
        [expert_ids.astype(f32), expert_slots.astype(f32), route_weight], axis=1
    ).T

    my_rows, away, routes = attention(
        queries, keys, values, level_index, level_table, out_weight, my_tokens, route
    )
    for hop in range(1, n_sub):
        my_rows = my_rows + moved(away[hop - 1], "sub", hop).astype(f32)
    shared = my_rows.astype(bf16)
    total = shared.astype(f32)
    for hop in range(1, n_head):
        total = total + moved(shared, "head", hop).astype(f32)
    stream = residual.astype(f32) + total
    mean_square = jnp.mean(stream * stream, axis=-1, keepdims=True)
    normed = (stream * lax.rsqrt(mean_square + 1e-06) * norm_gain).astype(bf16)

    width = D // n_head
    capacity = 3 * (my_tokens * TOPK // EXPERTS) // 2
    exp_here = w_gate_up.shape[0]
    all_tokens = routes.shape[1]
    first = (my_seq * n_sub + my_sub) * exp_here
    stream_part = lax.dynamic_slice_in_dim(stream, my_head * width, width, 1)

    def part_of(value, side):
        return lax.dynamic_slice_in_dim(value, (my_head - side) % n_head * width, width, 1)

    mine = part_of(normed, 0)
    if all_tokens * D * 2 <= FUSED_BYTES:
        blocks = [[part_of(normed, side) for side in range(n_head)]]
        for hop in range(1, n_seq):
            part = moved(mine, "seq", hop)
            blocks.append([part] + [moved(part, "head", side) for side in range(1, n_head)])
        pieces = [piece for block in blocks for piece in block]
        pieces = pieces + [
            moved(piece, "sub", hop) for hop in range(1, n_sub) for piece in pieces
        ]
        results = run_fused(routes, pieces, w_gate_up, w_down, n_head, n_sub, capacity)

        def reduced(side):
            value = results[side]
            for hop in range(1, n_sub):
                value = value + moved(results[hop * n_head + side], "sub", -hop).astype(f32)
            return [
                value[hop * my_tokens : (hop + 1) * my_tokens].astype(bf16 if side else f32)
                for hop in range(n_seq)
            ]

        order = [*range(1, n_seq), 0]
        others = [lax.optimization_barrier(reduced(side)) for side in range(1, n_head)]
        owns = lax.optimization_barrier(reduced(0))
        expert_sum = 0.0
        for hop in order:
            own = owns[hop]
            for side in range(1, n_head):
                own = own + moved(others[side - 1][hop], "head", side).astype(f32)
            if hop:
                own = moved(own.astype(bf16), "seq", -hop).astype(f32)
            expert_sum = expert_sum + own
        return (stream_part + expert_sum).astype(bf16)

    step = max(1, n_seq // 4)
    gathered = [normed]
    for begin in range(1, n_seq, step):
        hops = range(begin, min(begin + step, n_seq))
        part = jnp.concatenate([moved(mine, "seq", hop) for hop in hops], axis=0)
        joined = jnp.zeros((n_head, part.shape[0], width), bf16)
        parts = [part] + [moved(part, "head", side) for side in range(1, n_head)]
        for side, piece in enumerate(parts):
            joined = lax.dynamic_update_index_in_dim(joined, piece, (my_head - side) % n_head, 0)
        gathered.append(jnp.transpose(joined, (1, 0, 2)).reshape(-1, D))
    here = jnp.concatenate(gathered, axis=0)

    named, slots, weights = jnp.split(routes, 3, axis=0)
    count = all_tokens // my_tokens * capacity
    local = (first + jnp.arange(exp_here, dtype=jnp.int32)).astype(f32)
    block_of = (jnp.arange(all_tokens, dtype=jnp.int32) // my_tokens * capacity).astype(f32)
    place, share = routed(named[None], slots[None], weights[None], local[:, None, None], block_of)
    row = jnp.arange(count, dtype=jnp.int32).astype(f32)
    chosen = place == row[None, :, None]
    scale = jnp.sum(jnp.where(chosen, share, 0.0), axis=2, keepdims=True)
    pick = chosen.astype(bf16).reshape(exp_here * count, all_tokens)
    picks = jnp.split(pick, n_sub, axis=1)
    rows = dot(picks[0], here)
    for hop in range(1, n_sub):
        rows = rows + dot(picks[hop], moved(here, "sub", hop))
    rows = rows.astype(bf16).reshape(exp_here, count, D)
    pieces = run_experts(rows, w_gate_up, w_down, scale).reshape(-1, D)

    def combined(part):
        return dot(part, pieces, ((0,), (0,)))

    sent = [moved(combined(picks[hop]).astype(bf16), "sub", -hop) for hop in range(1, n_sub)]
    merged = combined(picks[0])
    for value in sent:
        merged = merged + value.astype(f32)
    by_head = merged.reshape(n_seq, my_tokens, n_head, width)
    expert_sum = 0.0
    for begin in range(0, n_seq, step):
        hops = range(begin, min(begin + step, n_seq))
        group = by_head[begin : hops[-1] + 1]
        own = lax.dynamic_index_in_dim(group, my_head, 2, keepdims=False)
        for side in range(1, n_head):
            away = lax.dynamic_index_in_dim(group, (my_head + side) % n_head, 2, keepdims=False)
            own = own + moved(away.astype(bf16), "head", side).astype(f32)
        for place_in, hop in enumerate(hops):
            value = own[place_in]
            if hop:
                value = moved(value.astype(bf16), "seq", -hop).astype(f32)
            expert_sum = expert_sum + value
    return (stream_part + expert_sum).astype(bf16)


def solution(mesh):
    return jax.shard_map(
        on_device,
        mesh=mesh,
        in_specs=(
            P(("groups", "seq"), ("head", "sub")),
            P(("groups", "seq"), ("head", "sub")),
            P(("groups", "seq"), ("head", "sub")),
            P(("groups", "seq"), None),
            P(None, ("head", "sub")),
            P(("head", "sub"), None),
            P(("groups", "seq", "sub"), None),
            P(),
            P(("groups", "seq", "sub"), None),
            P(("groups", "seq", "sub"), None),
            P(("groups", "seq", "sub"), None),
            P(("seq", "sub"), None, None, "head"),
            P(("seq", "sub"), "head", None),
        ),
        out_specs=P(("groups", "seq", "sub"), "head"),
        check_vma=False,
    )
```

```python
import functools

import jax
import jax.numpy as jnp
from jax import lax
from jax.experimental import pallas as pl
from jax.experimental.pallas import tpu as pltpu
from jax.sharding import PartitionSpec as P

D = 2048
HEAD_DIM = 128
EXPERTS = 64
TOPK = 8
LOCAL_LEVELS = 8
FUSED_BYTES = 4 << 20

bf16, f32 = jnp.bfloat16, jnp.float32
SMEM = pltpu.MemorySpace.SMEM
VMEM = pltpu.MemorySpace.VMEM
HBM = pltpu.MemorySpace.HBM


def moved(value, axis, distance):
    size = lax.axis_size(axis)
    pairs = [(source, (source + distance) % size) for source in range(size)]
    return lax.ppermute(value, axis, pairs)


def swapped(value, axis, distance, upward):
    mask = 2**distance
    pairs = [(s, s ^ mask) for s in range(lax.axis_size(axis)) if not (upward and s & mask)]
    return lax.ppermute(value, axis, pairs)


def dot(a, b, contract=((1,), (0,))):
    return lax.dot_general(a, b, (contract, ((), ())), preferred_element_type=f32)


def bit_length(numbers, digits):
    counted = jnp.zeros_like(numbers)
    for place_bit in range(digits):
        counted = counted + (numbers >= 1 << place_bit).astype(jnp.int32)
    return counted


def columns(head):
    return slice(head * HEAD_DIM, (head + 1) * HEAD_DIM)


def looked_up(index, table_ref, head):
    weight = jnp.zeros(index.shape, f32)
    for entry in range(table_ref.shape[1]):
        weight = jnp.where(index == float(entry), table_ref[head, entry], weight)
    return weight


def load_all(sources, targets, sems):
    copies = [
        pltpu.make_async_copy(source, target, sems.at[number])
        for number, (source, target) in enumerate(zip(sources, targets))
    ]
    for copy in copies:
        copy.start()
    return copies


def state_kernel(keys_hbm, values_hbm, out_ref, keys_ref, values_ref, sems):
    for copy in load_all((keys_hbm, values_hbm), (keys_ref, values_ref), sems):
        copy.wait()
    for head in range(out_ref.shape[0]):
        span = columns(head)
        out_ref[head] = dot(keys_ref[:, span], values_ref[:, span], ((0,), (0,))).astype(bf16)


def within_kernel(n_loads, table_ref, *rest):
    sources = rest[:n_loads]
    out_ref, weight_ref, route_ref = rest[n_loads : n_loads + 3]
    kept_refs = rest[n_loads + 3 : n_loads + 6]
    scratch_refs, sems = rest[n_loads + 6 : -1], rest[-1]
    queries_ref = kept_refs[0]
    keys_ref, index_ref, values_ref, ids_ref, slots_ref, share_ref = scratch_refs
    targets = (queries_ref, *scratch_refs, *kept_refs[1:])
    copies = load_all(sources, targets, sems)
    for copy in copies[:7]:
        copy.wait()
    route_ref[0:TOPK, :] = ids_ref[...].astype(f32)
    route_ref[TOPK : 2 * TOPK, :] = slots_ref[...].astype(f32)
    route_ref[2 * TOPK : 3 * TOPK, :] = share_ref[...]
    block = queries_ref.shape[0]
    heads = queries_ref.shape[1] // HEAD_DIM
    levels = weight_ref.shape[1] // heads
    my_block = lax.axis_index("seq")
    rows = lax.broadcasted_iota(jnp.int32, (block, block), 0)
    cols = lax.broadcasted_iota(jnp.int32, (block, block), 1)
    depth = jnp.where(cols <= rows, bit_length(rows ^ cols, LOCAL_LEVELS), -1)
    index = index_ref[...].astype(f32).T
    for head in range(heads):
        span = columns(head)
        weight = looked_up(index, table_ref, head)
        mix = jnp.zeros((block, block), f32)
        for level in range(LOCAL_LEVELS):
            mix = jnp.where(depth == level, weight[:, level : level + 1], mix)
        scores = dot(queries_ref[:, span], keys_ref[:, span], ((1,), (1,)))
        mixed = (scores * mix).astype(bf16)
        out_ref[:, span] = dot(mixed, values_ref[:, span])
        for level in range(levels):
            owned = (my_block >> level & 1).astype(f32)
            column, slot = LOCAL_LEVELS + level, head * levels + level
            weight_ref[:, slot : slot + 1] = weight[:, column : column + 1] * owned
    for copy in copies[7:]:
        copy.wait()


def project_kernel(n_levels, weight_hbm, within_ref, queries_ref, level_ref, *rest):
    state_refs = rest[:n_levels]
    own_ref, away_ref, attended_ref, weight_ref, sems = rest[n_levels:]
    chunks = sems.shape[0]
    step = weight_ref.shape[1] // chunks
    spans = [slice(chunk * step, (chunk + 1) * step) for chunk in range(chunks)]
    copies = load_all(
        [weight_hbm.at[:, span] for span in spans], [weight_ref.at[:, span] for span in spans], sems
    )
    for head in range(queries_ref.shape[1] // HEAD_DIM):
        span = columns(head)
        total = within_ref[:, span]
        joined = jnp.concatenate([ref[head] for ref in state_refs], axis=1)
        reads = dot(queries_ref[:, span], joined)
        for level in range(n_levels):
            slot = head * n_levels + level
            total = total + level_ref[:, slot : slot + 1] * reads[:, columns(level)]
        attended_ref[:, span] = (total * HEAD_DIM ** (-0.5)).astype(bf16)
    tokens = own_ref.shape[0]
    n_sub = away_ref.shape[0] + 1
    my_sub = lax.axis_index("sub")
    for span, copy in zip(spans, copies):
        copy.wait()
        for hop in range(n_sub):
            start = pl.multiple_of((my_sub + hop) % n_sub * tokens, tokens)
            value = dot(attended_ref[pl.ds(start, tokens), :], weight_ref[:, span])
            if hop:
                away_ref[hop - 1, :, span] = value.astype(bf16)
            else:
                own_ref[:, span] = value


def pinned(values):
    return [pltpu.with_memory_space_constraint(value, HBM) for value in values]


def grant(mebibytes):
    return pltpu.CompilerParams(vmem_limit_bytes=mebibytes << 20)


def whole(shape):
    return pl.BlockSpec(shape, lambda *_: (0,) * len(shape))


def scalars():
    return pl.BlockSpec(memory_space=SMEM)


def attention(
    queries,
    keys,
    values,
    level_index,
    level_table,
    out_weight,
    residual,
    norm_gain,
    expert_ids,
    expert_slots,
    route_weight,
):
    block, width = queries.shape
    heads = width // HEAD_DIM
    my_tokens = residual.shape[0]
    n_seq, n_sub = lax.axis_size("seq"), lax.axis_size("sub")
    in_hbm = pl.BlockSpec(memory_space=HBM)
    in_vmem = pl.BlockSpec(memory_space=VMEM)
    state = pl.pallas_call(
        state_kernel,
        in_specs=[in_hbm] * 2,
        out_specs=in_vmem,
        out_shape=jax.ShapeDtypeStruct((heads, HEAD_DIM, HEAD_DIM), bf16),
        scratch_shapes=[pltpu.VMEM(keys.shape, bf16)] * 2 + [pltpu.SemaphoreType.DMA((2,))],
        compiler_params=grant(4),
    )(*pinned([keys, values]))
    levels = n_seq.bit_length() - 1
    scratch = [keys, level_index.T, values, expert_ids.T, expert_slots.T, route_weight.T]
    kept = [residual, norm_gain]
    loads = [queries, *scratch, *kept]
    within, level_weight, route, queries, residual, norm_gain = pl.pallas_call(
        functools.partial(within_kernel, len(loads)),
        in_specs=[scalars()] + [in_hbm] * len(loads),
        out_specs=[in_vmem] * 6,
        out_shape=[
            jax.ShapeDtypeStruct((block, width), f32),
            jax.ShapeDtypeStruct((block, heads * levels), f32),
            jax.ShapeDtypeStruct((3 * TOPK, my_tokens), f32),
        ]
        + [jax.ShapeDtypeStruct(value.shape, value.dtype) for value in [queries, *kept]],
        scratch_shapes=[pltpu.VMEM(value.shape, value.dtype) for value in scratch]
        + [pltpu.SemaphoreType.DMA((len(loads),))],
        compiler_params=grant(16),
    )(level_table.T, *pinned(loads))
    running = state.astype(f32)
    found = []
    for level in range(levels):
        sent = running.astype(bf16)
        last = level == levels - 1
        if last:
            sent, within, level_weight, route = lax.optimization_barrier(
                (sent, within, level_weight, route)
            )
        partner = swapped(sent, "seq", level, last)
        found.append(partner)
        running = running + partner.astype(f32)
    routes = [route] + [moved(route, "seq", hop) for hop in range(1, n_seq)]
    routes = jnp.concatenate(routes, axis=1)
    routes = jnp.concatenate([routes] + [moved(routes, "sub", hop) for hop in range(1, n_sub)], axis=1)
    found[-1], routes = lax.optimization_barrier((found[-1], routes))
    out_width = out_weight.shape[1]
    own, away = pl.pallas_call(
        functools.partial(project_kernel, levels),
        in_specs=[in_hbm] + [in_vmem] * (3 + levels),
        out_specs=[in_vmem] * 2,
        out_shape=[
            jax.ShapeDtypeStruct((my_tokens, out_width), f32),
            jax.ShapeDtypeStruct((n_sub - 1, my_tokens, out_width), bf16),
        ],
        scratch_shapes=[
            pltpu.VMEM((block, width), bf16),
            pltpu.VMEM((width, out_width), bf16),
            pltpu.SemaphoreType.DMA((4,)),
        ],
        compiler_params=grant(12),
    )(*pinned([out_weight]), within, queries, level_weight, *found)
    return own, away, routes, residual, norm_gain


def swiglu(gate, up):
    return (gate / (1.0 + jnp.exp(-gate)) * up).astype(bf16)


def expert_kernel(rows_ref, gate_up_ref, down_ref, scale_ref, out_ref):
    pair = jnp.swapaxes(gate_up_ref[0], 0, 1)
    rows = rows_ref[0]
    active = swiglu(dot(rows, pair[0]), dot(rows, pair[1]))
    out_ref[0] = (dot(active, down_ref[0]) * scale_ref[0]).astype(bf16)


def run_experts(rows, w_gate_up, w_down, scale):
    experts, count, width = rows.shape
    hidden = w_down.shape[1]
    return pl.pallas_call(
        expert_kernel,
        grid=(experts,),
        in_specs=[
            pl.BlockSpec((1, count, width), lambda e: (e, 0, 0)),
            pl.BlockSpec((1, width, 2, hidden), lambda e: (e, 0, 0, 0)),
            pl.BlockSpec((1, hidden, width), lambda e: (e, 0, 0)),
            pl.BlockSpec((1, count, 1), lambda e: (e, 0, 0)),
        ],
        out_specs=pl.BlockSpec((1, count, width), lambda e: (e, 0, 0)),
        out_shape=jax.ShapeDtypeStruct(rows.shape, bf16),
    )(rows, w_gate_up, w_down, scale)


def routed(named, slots, weights, expert, slot_base):
    match = (named == expert) & (slots >= 0)
    place = jnp.sum(jnp.where(match, slots + slot_base + 1.0, 0.0), axis=-2, keepdims=True) - 1.0
    share = jnp.sum(jnp.where(match, weights, 0.0), axis=-2, keepdims=True)
    return place, share


def gate_kernel(n_pieces, n_sub, capacity, head_ref, routes_ref, *rest):
    piece_refs = rest[:n_pieces]
    gate_up_ref, gate_ref, up_ref, pick_ref, scale_ref, tokens_ref, rows_ref = rest[n_pieces:]
    step = pl.program_id(0)
    experts, count = scale_ref.shape[0], scale_ref.shape[1]
    all_tokens = routes_ref.shape[1]

    @pl.when(step == 0)
    def _():
        first = (lax.axis_index("seq") * n_sub + lax.axis_index("sub")) * experts
        size = piece_refs[0].shape[0]
        for block, ref in enumerate(piece_refs):
            tokens_ref[block * size : (block + 1) * size, :] = ref[...]
        named = routes_ref[0:TOPK, :]
        slots = routes_ref[TOPK : 2 * TOPK, :]
        weights = routes_ref[2 * TOPK : 3 * TOPK, :]
        lane = lax.broadcasted_iota(jnp.int32, (1, all_tokens), 1)
        slot_base = (lane // size * capacity).astype(f32)
        row = lax.broadcasted_iota(jnp.int32, (count, all_tokens), 0).astype(f32)
        for expert in range(experts):
            name = (first + expert).astype(f32)
            place, share = routed(named, slots, weights, name, slot_base)
            chosen = place == row
            scale_ref[expert] = jnp.sum(jnp.where(chosen, share, 0.0), axis=1, keepdims=True)
            pick_ref[expert * count : (expert + 1) * count, :] = jnp.where(
                chosen, 1.0, 0.0
            ).astype(bf16)
        rows_ref[...] = dot(pick_ref[...], tokens_ref[...]).astype(bf16)

    rows = rows_ref[pl.ds(pl.multiple_of(step * count, count), count), :]
    pair = jnp.swapaxes(gate_up_ref[0], 0, 1)
    gate_ref[0] = dot(rows, pair[0])
    up_ref[0] = dot(rows, pair[1])


def finish_kernel(n_head, n_sub, n_blocks, head_ref, *rest):
    sides = n_head - 1
    piece_refs = rest[: sides * n_blocks]
    gate_up_refs = rest[sides * n_blocks : sides * (n_blocks + 1)]
    gate_ref, up_ref, down_ref, pick_ref, scale_ref = rest[sides * (n_blocks + 1) :][:5]
    out_refs = rest[sides * (n_blocks + 1) + 5 : -3]
    tokens_ref, rows_ref, result_ref = rest[-3:]
    step = pl.program_id(0)
    experts, count = scale_ref.shape[0], scale_ref.shape[1]
    width = tokens_ref.shape[1]
    my_head = lax.axis_index("head")

    @pl.when(step == 0)
    def _():
        size = piece_refs[0].shape[0]
        for side in range(sides):
            for block in range(n_blocks):
                ref = piece_refs[side * n_blocks + block]
                tokens_ref[block * size : (block + 1) * size, :] = ref[...]
            rows_ref[side] = dot(pick_ref[...], tokens_ref[...]).astype(bf16)

    start = pl.multiple_of(step * count, count)
    gate, up = gate_ref[0], up_ref[0]
    for side in range(sides):
        pair = jnp.swapaxes(gate_up_refs[side][0], 0, 1)
        rows = rows_ref[side, pl.ds(start, count), :]
        gate = gate + dot(rows, pair[0])
        up = up + dot(rows, pair[1])
    piece = (dot(swiglu(gate, up), down_ref[0]) * scale_ref[step]).astype(bf16)
    for part in range(n_head):
        result_ref[part, pl.ds(start, count), :] = piece[:, part * width : (part + 1) * width]

    @pl.when(step == experts - 1)
    def _():
        tokens = pick_ref.shape[1] // n_sub
        for number, ref in enumerate(out_refs):
            hop, side = divmod(number, n_head)
            part = (my_head + side) % n_head
            pick = pick_ref[:, hop * tokens : (hop + 1) * tokens]
            ref[...] = dot(pick, result_ref[part], ((0,), (0,))).astype(ref.dtype)


def run_split(routes, pieces, w_gate_up, w_down, n_head, n_sub, capacity):
    experts, full, _, hidden = w_gate_up.shape
    size, width = pieces[0].shape
    blocks = len(pieces) // n_head
    all_tokens = routes.shape[1]
    tokens = all_tokens // n_sub
    count = all_tokens // size * capacity
    sides = n_head - 1
    head = lax.axis_index("head").astype(jnp.int32).reshape(1)

    def columns_of(side):
        return pl.BlockSpec(
            (1, width, 2, hidden), lambda e, head_ref: (e, (head_ref[0] + n_head - side) % n_head, 0, 0)
        )

    w_gate_up, w_down = pinned([w_gate_up, w_down])
    half = pl.BlockSpec((1, count, hidden), lambda e, head_ref: (e, 0, 0))
    halves = jax.ShapeDtypeStruct((experts, count, hidden), f32)
    gate, up, pick, scale = pl.pallas_call(
        functools.partial(gate_kernel, blocks, n_sub, capacity),
        grid_spec=pltpu.PrefetchScalarGridSpec(
            num_scalar_prefetch=1,
            grid=(experts,),
            in_specs=[whole(routes.shape)] + [whole((size, width))] * blocks + [columns_of(0)],
            out_specs=[half, half, whole((experts * count, all_tokens)), whole((experts, count, 1))],
            scratch_shapes=[
                pltpu.VMEM((all_tokens, width), bf16),
                pltpu.VMEM((experts * count, width), bf16),
            ],
        ),
        out_shape=[
            halves,
            halves,
            jax.ShapeDtypeStruct((experts * count, all_tokens), bf16),
            jax.ShapeDtypeStruct((experts, count, 1), f32),
        ],
        compiler_params=grant(24),
    )(head, routes, *pieces[::n_head], w_gate_up)
    others = [piece for side in range(1, n_head) for piece in pieces[side::n_head]]
    dtypes = [f32] * n_head + [bf16] * (n_head * (n_sub - 1))
    return pl.pallas_call(
        functools.partial(finish_kernel, n_head, n_sub, blocks),
        grid_spec=pltpu.PrefetchScalarGridSpec(
            num_scalar_prefetch=1,
            grid=(experts,),
            in_specs=[whole((size, width))] * len(others)
            + [columns_of(side) for side in range(1, n_head)]
            + [
                half,
                half,
                pl.BlockSpec((1, hidden, full), lambda e, head_ref: (e, 0, 0)),
                whole((experts * count, all_tokens)),
                whole((experts, count, 1)),
            ],
            out_specs=[whole((tokens, width))] * len(dtypes),
            scratch_shapes=[
                pltpu.VMEM((all_tokens, width), bf16),
                pltpu.VMEM((sides, experts * count, width), bf16),
                pltpu.VMEM((n_head, experts * count, width), bf16),
            ],
        ),
        out_shape=[jax.ShapeDtypeStruct((tokens, width), dtype) for dtype in dtypes],
        compiler_params=grant(36),
    )(head, *others, *[w_gate_up] * sides, gate, up, w_down, pick, scale)


def on_device(
    queries,
    keys,
    values,
    level_index,
    level_table,
    out_weight,
    residual,
    norm_gain,
    expert_ids,
    expert_slots,
    route_weight,
    w_gate_up,
    w_down,
):
    n_seq, n_head, n_sub = (lax.axis_size(name) for name in ("seq", "head", "sub"))
    my_seq, my_head, my_sub = (lax.axis_index(name) for name in ("seq", "head", "sub"))
    my_tokens = residual.shape[0]
    my_rows, away, routes, residual, norm_gain = attention(
        queries,
        keys,
        values,
        level_index,
        level_table,
        out_weight,
        residual,
        norm_gain,
        expert_ids,
        expert_slots,
        route_weight,
    )
    for hop in range(1, n_sub):
        my_rows = my_rows + moved(away[hop - 1], "sub", hop).astype(f32)
    shared = my_rows.astype(bf16)
    total = shared.astype(f32)
    for hop in range(1, n_head):
        total = total + moved(shared, "head", hop).astype(f32)
    stream = residual.astype(f32) + total
    mean_square = jnp.mean(stream * stream, axis=-1, keepdims=True)
    normed = (stream * lax.rsqrt(mean_square + 1e-06) * norm_gain).astype(bf16)

    width = D // n_head
    capacity = 3 * (my_tokens * TOPK // EXPERTS) // 2
    exp_here = w_gate_up.shape[0]
    all_tokens = routes.shape[1]
    first = (my_seq * n_sub + my_sub) * exp_here
    stream_part = lax.dynamic_slice_in_dim(stream, my_head * width, width, 1)

    def part_of(value, side):
        return lax.dynamic_slice_in_dim(value, (my_head - side) % n_head * width, width, 1)

    mine = part_of(normed, 0)
    if all_tokens * D * 2 <= FUSED_BYTES:
        blocks = [[part_of(normed, side) for side in range(n_head)]]
        for hop in range(1, n_seq):
            part = moved(mine, "seq", hop)
            blocks.append([part] + [moved(part, "head", side) for side in range(1, n_head)])
        pieces = [piece for block in blocks for piece in block]
        pieces = pieces + [
            moved(piece, "sub", hop) for hop in range(1, n_sub) for piece in pieces
        ]
        results = run_split(routes, pieces, w_gate_up, w_down, n_head, n_sub, capacity)

        def reduced(side):
            value = results[side]
            for hop in range(1, n_sub):
                value = value + moved(results[hop * n_head + side], "sub", -hop).astype(f32)
            return [
                value[hop * my_tokens : (hop + 1) * my_tokens].astype(bf16 if side else f32)
                for hop in range(n_seq)
            ]

        order = [*range(1, n_seq), 0]
        others = [lax.optimization_barrier(reduced(side)) for side in range(1, n_head)]
        owns = lax.optimization_barrier(reduced(0))
        expert_sum = 0.0
        for hop in order:
            own = owns[hop]
            for side in range(1, n_head):
                own = own + moved(others[side - 1][hop], "head", side).astype(f32)
            if hop:
                own = moved(own.astype(bf16), "seq", -hop).astype(f32)
            expert_sum = expert_sum + own
        return (stream_part + expert_sum).astype(bf16)

    step = max(1, n_seq // 4)
    gathered = [normed]
    for begin in range(1, n_seq, step):
        hops = range(begin, min(begin + step, n_seq))
        part = jnp.concatenate([moved(mine, "seq", hop) for hop in hops], axis=0)
        joined = jnp.zeros((n_head, part.shape[0], width), bf16)
        parts = [part] + [moved(part, "head", side) for side in range(1, n_head)]
        for side, piece in enumerate(parts):
            joined = lax.dynamic_update_index_in_dim(joined, piece, (my_head - side) % n_head, 0)
        gathered.append(jnp.transpose(joined, (1, 0, 2)).reshape(-1, D))
    here = jnp.concatenate(gathered, axis=0)

    named, slots, weights = jnp.split(routes, 3, axis=0)
    count = all_tokens // my_tokens * capacity
    local = (first + jnp.arange(exp_here, dtype=jnp.int32)).astype(f32)
    block_of = (jnp.arange(all_tokens, dtype=jnp.int32) // my_tokens * capacity).astype(f32)
    place, share = routed(named[None], slots[None], weights[None], local[:, None, None], block_of)
    row = jnp.arange(count, dtype=jnp.int32).astype(f32)
    chosen = place == row[None, :, None]
    scale = jnp.sum(jnp.where(chosen, share, 0.0), axis=2, keepdims=True)
    pick = chosen.astype(bf16).reshape(exp_here * count, all_tokens)
    picks = jnp.split(pick, n_sub, axis=1)
    rows = dot(picks[0], here)
    for hop in range(1, n_sub):
        rows = rows + dot(picks[hop], moved(here, "sub", hop))
    rows = rows.astype(bf16).reshape(exp_here, count, D)
    pieces = run_experts(rows, w_gate_up, w_down, scale).reshape(-1, D)

    def combined(part):
        return dot(part, pieces, ((0,), (0,)))

    sent = [moved(combined(picks[hop]).astype(bf16), "sub", -hop) for hop in range(1, n_sub)]
    merged = combined(picks[0])
    for value in sent:
        merged = merged + value.astype(f32)
    by_head = merged.reshape(n_seq, my_tokens, n_head, width)
    expert_sum = 0.0
    for begin in range(0, n_seq, step):
        hops = range(begin, min(begin + step, n_seq))
        group = by_head[begin : hops[-1] + 1]
        own = lax.dynamic_index_in_dim(group, my_head, 2, keepdims=False)
        for side in range(1, n_head):
            away = lax.dynamic_index_in_dim(group, (my_head + side) % n_head, 2, keepdims=False)
            own = own + moved(away.astype(bf16), "head", side).astype(f32)
        for place_in, hop in enumerate(hops):
            value = own[place_in]
            if hop:
                value = moved(value.astype(bf16), "seq", -hop).astype(f32)
            expert_sum = expert_sum + value
    return (stream_part + expert_sum).astype(bf16)


def solution(mesh):
    return jax.shard_map(
        on_device,
        mesh=mesh,
        in_specs=(
            P(("groups", "seq"), ("head", "sub")),
            P(("groups", "seq"), ("head", "sub")),
            P(("groups", "seq"), ("head", "sub")),
            P(("groups", "seq"), None),
            P(None, ("head", "sub")),
            P(("head", "sub"), None),
            P(("groups", "seq", "sub"), None),
            P(),
            P(("groups", "seq", "sub"), None),
            P(("groups", "seq", "sub"), None),
            P(("groups", "seq", "sub"), None),
            P(("seq", "sub"), None, None, "head"),
            P(("seq", "sub"), "head", None),
        ),
        out_specs=P(("groups", "seq", "sub"), "head"),
        check_vma=False,
    )
```
